256 devices in a mesh: qt: 4 (over y), kt: 8 (over z_hi, x), hd: 8 (over z_lo, core).
Axes of the slice: x: 4, y: 4, z: 8 (z_hi: 2, z_lo: 4; z = z_hi * 4 + z_lo), core: 2. Of those that a mesh axis runs over, the one named last changes fastest.
Arguments:
- query_proj: bfloat16 [4096, 8192], P(('qt', 'kt'), 'hd'), may hold values from -6 to 6
- key_proj: bfloat16 [4096, 1024], P(('qt', 'kt'), 'hd'), may hold values from -6 to 6
- value_proj: bfloat16 [4096, 1024], P(('qt', 'kt'), 'hd'), may hold values from -6 to 6
- out_grad: bfloat16 [4096, 8192], P(('qt', 'kt'), 'hd'), may hold values from -6 to 6
- log_norm: float32 [64, 4096], P('hd', ('qt', 'kt')), may hold values from -500 to 500, as said below
- row_delta: float32 [64, 4096], P('hd', ('qt', 'kt')), may hold values from -5000 to 5000, as said below
- first_key: int32 [4096], P(('qt', 'kt')), may hold values from 0 to 512, as said below
- tile_pairs: int32 [379, 2], replicated, may hold values from 0 to 31, as said below
- hidden: bfloat16 [4096, 8192], P(('qt', 'kt'), 'hd'), may hold values from -6 to 6
- adapter_down: bfloat16 [8192, 128], P('hd'), may hold values from -0.0625 to 0.0625
- adapter_up: bfloat16 [2, 64, 1024], P(None, None, 'hd'), may hold values from -0.75 to 0.75
Outputs:
- query_grad: bfloat16 [4096, 8192], P(('qt', 'kt'), 'hd')
- down_factor_gradient: float32 [8192, 128], P('hd')
- up_factor_gradient: float32 [2, 64, 1024], P(None, None, 'hd')
The draws below stay inside these ranges and needn't reach their ends.
Inputs may be any that keep to these rules, and one draw needn't show every extreme that they name: log_norm[a, t] is the logarithm of the sum over the allowed keys s of exp(scores[a, t, s]), as the forward pass computed it. row_delta[a, t] is the inner product of o_a[t] with the forward output of head a at row t, that output rounded to bfloat16. first_key[t] <= t; the window falls into exactly 4 runs of tokens with equal first_key, each run's first_key is the position of its first token, and the last run begins at position 512. `tile_pairs`: each row (a, b) names a query tile a and a key tile b of 128 tokens with b <= a; no row appears twice, and every pair (a, a) is a row.
All inputs are finite; a program needn't handle non-finite values.
Results may differ from the reference program's by a relative error of at most 0.009.
Values may be sent and summed in bfloat16 or wider, within the bound.
No kernel may reach another device: no remote copies, remote signals or barrier semaphores. Data moves between devices by JAX's collectives and lax.ppermute only.
A program may use at most 64 MiB of HBM per device.

```python
import math
import jax
import jax.numpy as jnp
from jax import lax

H = 64
KVH = 8
HD = 128
D = 8192
R = 64
TILE = 128
SEGS = 4
SEQ = 4096
EXTRA = 347
NPAIRS = 379


def draw_first_key(key, part):
    head_start = SEQ // 8
    order = jax.random.permutation(jax.random.fold_in(key, 31), head_start - 1) + 1
    cuts = jnp.concatenate([order[:SEGS - 2].astype(jnp.int32), jnp.full((1,), head_start, jnp.int32)])
    position = jnp.arange(SEQ, dtype=jnp.int32)
    below = jnp.where(cuts[None, :] <= position[:, None], cuts[None, :], 0)
    return jnp.max(below, axis=1).astype(jnp.int32)


def draw_tile_pairs(key, part):
    tile_count = SEQ // TILE
    cells = tile_count * tile_count
    grid_ids = jnp.arange(cells, dtype=jnp.int32)
    row_ids = grid_ids // tile_count
    col_ids = grid_ids % tile_count
    raw_scores = jax.random.randint(jax.random.fold_in(key, 41), (cells,), 0, 2 ** 30 // cells, dtype=jnp.int32)
    ranked = jnp.where(col_ids < row_ids, raw_scores * cells + grid_ids, -1)
    unused, picked = lax.top_k(ranked, EXTRA)
    chosen = jnp.stack([picked // tile_count, picked % tile_count], axis=1)
    diagonal = jnp.stack([jnp.arange(tile_count, dtype=jnp.int32), jnp.arange(tile_count, dtype=jnp.int32)], axis=1)
    joined = jnp.concatenate([diagonal, chosen.astype(jnp.int32)], axis=0)
    order = jax.random.permutation(jax.random.fold_in(key, 43), NPAIRS)
    return joined[order].astype(jnp.int32)


def float_field(key, salt_number, field_shape):
    values_drawn = jnp.clip(jax.random.normal(jax.random.fold_in(key, salt_number), field_shape, jnp.float32), -6.0, 6.0)
    return values_drawn.astype(jnp.bfloat16)


def draw_query_proj(key, part):
    return float_field(key, 100, (SEQ, H * HD))


def draw_key_proj(key, part):
    return float_field(key, 200, (SEQ, KVH * HD))


def draw_value_proj(key, part):
    return float_field(key, 300, (SEQ, KVH * HD))


def draw_out_grad(key, part):
    return float_field(key, 400, (SEQ, H * HD))


def forward_stats(key, part):
    query_all = draw_query_proj(key, part).astype(jnp.float32)
    key_all = draw_key_proj(key, part).astype(jnp.float32)
    value_all = draw_value_proj(key, part).astype(jnp.float32)
    grad_all = draw_out_grad(key, part).astype(jnp.float32)
    first_key = draw_first_key(key, part)
    tile_pairs = draw_tile_pairs(key, part)
    tile_count = SEQ // TILE
    tile_ids = jnp.arange(tile_count, dtype=jnp.int32)
    pair_query = (tile_pairs[:, 0:1] == tile_ids[None, :]).astype(jnp.float32)
    pair_key = (tile_pairs[:, 1:2] == tile_ids[None, :]).astype(jnp.float32)
    live = jnp.dot(pair_query.T, pair_key, precision=lax.Precision.HIGHEST) > 0.5
    position = jnp.arange(SEQ, dtype=jnp.int32)
    tile_of = position // TILE
    allowed = live[tile_of[:, None], tile_of[None, :]] & (position[None, :] <= position[:, None]) & (position[None, :] >= first_key[:, None])
    inv_root = 1.0 / math.sqrt(HD)
    group_size = H // KVH

    def one_head(head):
        kv_head = head // group_size
        query_part = lax.dynamic_slice_in_dim(query_all, head * HD, HD, 1)
        grad_part = lax.dynamic_slice_in_dim(grad_all, head * HD, HD, 1)
        key_part = lax.dynamic_slice_in_dim(key_all, kv_head * HD, HD, 1)
        value_part = lax.dynamic_slice_in_dim(value_all, kv_head * HD, HD, 1)
        scores = jnp.dot(query_part, key_part.T, precision=lax.Precision.HIGHEST) * inv_root
        highest = jnp.max(jnp.where(allowed, scores, -1e+30), axis=1, keepdims=True)
        weights = jnp.where(allowed, jnp.exp(scores - highest), 0.0)
        totals = jnp.sum(weights, axis=1, keepdims=True)
        log_total = highest[:, 0] + jnp.log(totals[:, 0])
        output = jnp.dot(weights / totals, value_part, precision=lax.Precision.HIGHEST)
        output_low = output.astype(jnp.bfloat16).astype(jnp.float32)
        delta_rows = jnp.sum(grad_part * output_low, axis=1)
        return (log_total, delta_rows)
    return lax.map(one_head, jnp.arange(H, dtype=jnp.int32))


def draw_log_norm(key, part):
    log_all, delta_all = forward_stats(key, part)
    return log_all.astype(jnp.float32)


def draw_row_delta(key, part):
    log_all, delta_all = forward_stats(key, part)
    return delta_all.astype(jnp.float32)


def steps_of(stream_key, dims, pieces, smallest, top_value):
    def one(dim, blocks):
        steps = jax.random.uniform(jax.random.fold_in(jax.random.fold_in(stream_key, 6), dim), (blocks,), jnp.float32, smallest / len(pieces), top_value / len(pieces))
        return jnp.repeat(jnp.exp(steps), dims[dim] // blocks).reshape((-1,) + (1,) * (len(dims) - dim - 1))

    factor_of = one(*pieces[0])
    for cut in pieces[1:]:
        factor_of = factor_of * one(*cut)
    return factor_of


def centred(key, extent, deviation, most, pieces=(), kind=jnp.bfloat16):
    level = steps_of(key, extent, pieces, -0.22, 0.18) if pieces else 1.0
    drawn = jax.random.normal(key, extent, jnp.float32) * deviation * level
    return jnp.minimum(jnp.maximum(drawn, -most), most).astype(kind)


def setup_inputs(seed: int = 0) -> dict:
    arg_keys = jax.random.split(jax.random.key(seed), 12)
    return {
        "query_proj": draw_query_proj(jax.random.fold_in(arg_keys[11], 71), 0),
        "key_proj": draw_key_proj(jax.random.fold_in(arg_keys[11], 71), 0),
        "value_proj": draw_value_proj(jax.random.fold_in(arg_keys[11], 71), 0),
        "out_grad": draw_out_grad(jax.random.fold_in(arg_keys[11], 71), 0),
        "log_norm": draw_log_norm(jax.random.fold_in(arg_keys[11], 71), 0),
        "row_delta": draw_row_delta(jax.random.fold_in(arg_keys[11], 71), 0),
        "first_key": draw_first_key(jax.random.fold_in(arg_keys[11], 71), 0),
        "tile_pairs": draw_tile_pairs(jax.random.fold_in(arg_keys[11], 71), 0),
        "hidden": centred(arg_keys[8], (SEQ, D), 1.0, 6.0, ((0, 32), (1, 8))),
        "adapter_down": centred(arg_keys[9], (D, 2 * R), D ** -0.5, 0.0625, ((0, 8),)),
        "adapter_up": centred(arg_keys[10], (2, R, KVH * HD), R ** -0.5, 0.75, ((2, 8),)),
    }


adapter_scale_factor = 0.25

def allowed_pairs(first_key, tile_pairs):
    tile_count = SEQ // TILE
    tile_ids = jnp.arange(tile_count, dtype=jnp.int32)
    pair_query = (tile_pairs[:, 0:1] == tile_ids[None, :]).astype(jnp.float32)
    pair_key = (tile_pairs[:, 1:2] == tile_ids[None, :]).astype(jnp.float32)
    live = jnp.dot(pair_query.T, pair_key, precision=lax.Precision.HIGHEST) > 0.5
    position = jnp.arange(SEQ, dtype=jnp.int32)
    tile_of = position // TILE
    inside = live[tile_of[:, None], tile_of[None, :]]
    causal = (position[None, :] <= position[:, None]) & (position[None, :] >= first_key[:, None])
    return inside & causal

def reference(query_proj, key_proj, value_proj, out_grad, log_norm, row_delta, first_key, tile_pairs, hidden, adapter_down, adapter_up):
    allowed = allowed_pairs(first_key, tile_pairs)
    group_size = H // KVH
    inv_root = 1.0 / math.sqrt(HD)
    query_heads = query_proj.astype(jnp.float32).reshape(SEQ, H, HD)
    grad_heads = out_grad.astype(jnp.float32).reshape(SEQ, H, HD)
    key_heads = key_proj.astype(jnp.float32).reshape(SEQ, KVH, HD)
    value_heads = value_proj.astype(jnp.float32).reshape(SEQ, KVH, HD)

    def one_head(head):
        kv_head = head // group_size
        query_part = lax.dynamic_index_in_dim(query_heads, head, 1, keepdims=False)
        grad_part = lax.dynamic_index_in_dim(grad_heads, head, 1, keepdims=False)
        key_part = lax.dynamic_index_in_dim(key_heads, kv_head, 1, keepdims=False)
        value_part = lax.dynamic_index_in_dim(value_heads, kv_head, 1, keepdims=False)
        log_part = lax.dynamic_index_in_dim(log_norm, head, 0, keepdims=False)
        delta_part = lax.dynamic_index_in_dim(row_delta, head, 0, keepdims=False)
        scores = jnp.dot(query_part, key_part.T, precision=lax.Precision.HIGHEST) * inv_root
        probs = jnp.where(allowed, jnp.exp(scores - log_part[:, None]), 0.0)
        probs_low = lax.optimization_barrier(probs.astype(jnp.bfloat16)).astype(jnp.float32)
        value_grad = jnp.dot(probs_low.T, grad_part, precision=lax.Precision.HIGHEST)
        dprobs = jnp.dot(grad_part, value_part.T, precision=lax.Precision.HIGHEST)
        dscores = probs * (dprobs - delta_part[:, None])
        dscores_low = lax.optimization_barrier(dscores.astype(jnp.bfloat16)).astype(jnp.float32)
        query_grad = jnp.dot(dscores_low, key_part, precision=lax.Precision.HIGHEST) * inv_root
        key_grad = jnp.dot(dscores_low.T, query_part, precision=lax.Precision.HIGHEST) * inv_root
        return (query_grad, key_grad, value_grad)
    query_all, key_all, value_all = lax.map(one_head, jnp.arange(H, dtype=jnp.int32))
    query_grad = jnp.transpose(query_all, (1, 0, 2)).reshape(SEQ, H * HD).astype(jnp.bfloat16)
    key_sum = key_all.reshape(KVH, group_size, SEQ, HD).sum(axis=1)
    value_sum = value_all.reshape(KVH, group_size, SEQ, HD).sum(axis=1)
    key_low = jnp.transpose(key_sum, (1, 0, 2)).reshape(SEQ, KVH * HD).astype(jnp.bfloat16)
    value_low = jnp.transpose(value_sum, (1, 0, 2)).reshape(SEQ, KVH * HD).astype(jnp.bfloat16)
    latent = jnp.dot(hidden, adapter_down, preferred_element_type=jnp.float32).astype(jnp.bfloat16)
    back_key = jnp.dot(key_low, adapter_up[0].T, preferred_element_type=jnp.float32)
    back_value = jnp.dot(value_low, adapter_up[1].T, preferred_element_type=jnp.float32)
    backward_pass = jnp.concatenate([back_key, back_value], axis=1).astype(jnp.bfloat16)
    down_factor_gradient = adapter_scale_factor * jnp.dot(hidden.T, backward_pass, preferred_element_type=jnp.float32)
    key_up_factor = jnp.dot(latent[:, :R].T, key_low, preferred_element_type=jnp.float32)
    value_up_factor = jnp.dot(latent[:, R:].T, value_low, preferred_element_type=jnp.float32)
    up_factor_gradient = adapter_scale_factor * jnp.stack([key_up_factor, value_up_factor])
    return (query_grad, down_factor_gradient, up_factor_gradient)
```

```python
import functools
import math

import jax
import jax.numpy as jnp
from jax import lax
from jax.experimental import pallas as pl
from jax.experimental.pallas import tpu as pltpu
from jax.sharding import PartitionSpec as P

HD = 128
R = 64
TILE = 128
HEADS = 8
NY = 4
NX = 4
NZ = 2
NKT = NX * NZ
NZLO = 4
NCORE = 2
LOG2E = math.log2(math.e)
INV_ROOT = 1.0 / math.sqrt(HD)
SCALE = 0.25
ROWS = 2 * TILE + 16

f32 = jnp.float32
bf16 = jnp.bfloat16


def attend_kernel(meta, p0, p1, p2, p3, kv, dkv, dq0, dq1, dq2, dq3, kt_sc, dk_sc, dv_sc, dq_sc):
    packed = (p0, p1, p2, p3)
    dqs = (dq0, dq1, dq2, dq3)
    contract_last = (((1,), (1,)), ((), ()))
    for t in range(NKT):
        kt_sc[t] = kv[t, 0:TILE, :].T
    dk_sc[...] = jnp.zeros_like(dk_sc)
    dv_sc[...] = jnp.zeros_like(dv_sc)
    row = lax.broadcasted_iota(jnp.int32, (TILE, TILE), 0)
    col = lax.broadcasted_iota(jnp.int32, (TILE, TILE), 1)
    key_base = meta[NY, 0]
    for s in range(NY):
        p = packed[s]
        dq_sc[...] = jnp.zeros_like(dq_sc)

        @pl.when(meta[NY, 1 + s] > 0)
        def _():
            rows = p[2 * TILE : ROWS, :].astype(f32)
            logs = rows[0:1] + rows[1:2] + rows[2:3]
            deltas = rows[3:4] + rows[4:5] + rows[5:6]
            first = (rows[6:7, 0:TILE] + rows[6:7, TILE : 2 * TILE]).astype(jnp.int32)
            query_pos = meta[NY + 1, s] * TILE + col

            def one_tile(t, carry):
                @pl.when(meta[s, t] > 0)
                def _():
                    key = kv[t, 0:TILE, :]
                    val = kv[t, TILE : 2 * TILE, :]
                    key_pos = (key_base + t) * TILE + row
                    allowed = (key_pos <= query_pos) & (key_pos >= first)
                    probs_low = []
                    dscores_low = []
                    for h in range(HEADS):
                        cols = slice(h * HD, (h + 1) * HD)
                        scores = lax.dot_general(key, p[0:TILE, cols], contract_last, preferred_element_type=f32)
                        dprobs = lax.dot_general(val, p[TILE : 2 * TILE, cols], contract_last, preferred_element_type=f32)
                        probs = jnp.where(allowed, jnp.exp2(scores * (INV_ROOT * LOG2E) - logs[:, cols]), 0.0)
                        dscores = probs * (dprobs - deltas[:, cols])
                        probs_low.append(probs.astype(bf16))
                        dscores_low.append(dscores.astype(bf16))
                    probs_all = jnp.concatenate(probs_low, axis=1)
                    dscores_all = jnp.concatenate(dscores_low, axis=1)
                    queries = jnp.concatenate([p[0:TILE, h * HD : (h + 1) * HD] for h in range(HEADS)], axis=0)
                    grads = jnp.concatenate([p[TILE : 2 * TILE, h * HD : (h + 1) * HD] for h in range(HEADS)], axis=0)
                    dv_sc[t] += jnp.dot(probs_all, grads, preferred_element_type=f32)
                    dk_sc[t] += jnp.dot(dscores_all, queries, preferred_element_type=f32)
                    dq_sc[...] += jnp.dot(kt_sc[t], dscores_all, preferred_element_type=f32)

                return carry

            lax.fori_loop(0, NKT, one_tile, 0)

        for h in range(HEADS):
            cols = slice(h * HD, (h + 1) * HD)
            dqs[s][:, cols] = (dq_sc[:, cols].T * INV_ROOT).astype(dqs[s].dtype)
    for t in range(NKT):
        dkv[t % NX, t // NX, 0] = (dk_sc[t] * INV_ROOT).astype(bf16)
        dkv[t % NX, t // NX, 1] = dv_sc[t].astype(bf16)


def attend(meta, packed, kv):
    vm = pl.BlockSpec(memory_space=pltpu.VMEM)
    return pl.pallas_call(
        attend_kernel,
        in_specs=[pl.BlockSpec(memory_space=pltpu.SMEM)] + [vm] * (NY + 1),
        out_specs=[vm] * (NY + 1),
        out_shape=[jax.ShapeDtypeStruct((NX, NZ, 2, TILE, HD), bf16), jax.ShapeDtypeStruct((TILE, HEADS * HD), f32)]
        + [jax.ShapeDtypeStruct((TILE, HEADS * HD), bf16)] * (NY - 1),
        scratch_shapes=[
            pltpu.VMEM((NKT, HD, TILE), bf16),
            pltpu.VMEM((NKT, TILE, HD), f32),
            pltpu.VMEM((NKT, TILE, HD), f32),
            pltpu.VMEM((HD, HEADS * TILE), f32),
        ],
        name="attend",
    )(meta, *packed, kv)


def split3(x):
    hi = lax.reduce_precision(x, 8, 7)
    rest = x - hi
    mid = lax.reduce_precision(rest, 8, 7)
    low = rest - mid
    return [hi.astype(bf16), mid.astype(bf16), low.astype(bf16)]


def groups(size, key):
    found = {}
    for i in range(size):
        found.setdefault(key(i), []).append(i)
    return list(found.values())


X_GROUPS = groups(NKT, lambda i: i // NX)
XY_GROUPS = groups(NY * NKT, lambda i: (i % NKT) // NX)
Z_GROUPS = groups(NKT * NZLO * NCORE, lambda i: ((i // (NZLO * NCORE)) % NX, i % NCORE))
Z_SWAP = [(i, i ^ NX) for i in range(NKT)]
CORE_SWAP = [(i, i ^ 1) for i in range(NZLO * NCORE)]


def body(
    query_proj,
    key_proj,
    value_proj,
    out_grad,
    log_norm,
    row_delta,
    first_key,
    tile_pairs,
    hidden,
    adapter_down,
    adapter_up,
):
    y = lax.axis_index("qt")
    kt = lax.axis_index("kt")
    z_hi = kt // NX
    core = lax.axis_index("hd") % NCORE

    first_hi = lax.reduce_precision(first_key.astype(f32), 8, 7)
    first_row = jnp.concatenate([first_hi, first_key.astype(f32) - first_hi, jnp.zeros((6 * TILE,), f32)])
    rows = (
        split3((log_norm * LOG2E).reshape(1, HEADS * TILE))
        + split3(row_delta.reshape(1, HEADS * TILE))
        + [first_row.astype(bf16).reshape(1, HEADS * TILE), jnp.zeros((9, HEADS * TILE), bf16)]
    )
    packed = jnp.concatenate([query_proj, out_grad] + rows, axis=0)
    shifts = [(1, [(i, i + 1 - NY) for i in range(NY - 1, NY)]), (2, [(2, 0), (3, 1)]), (3, [(1, 0), (2, 1), (3, 2)])]
    blocks = {0: packed}
    for s, perm in reversed(shifts):
        blocks[s] = lax.ppermute(packed, "qt", perm)

    kv = jnp.concatenate([key_proj, value_proj], axis=0)
    kv = lax.all_to_all(jnp.broadcast_to(kv[None], (NKT, 2 * TILE, HD)), "kt", 0, 0, tiled=True)

    tile_count = NY * NKT
    tile_ids = jnp.arange(tile_count, dtype=jnp.int32)
    src = (y - jnp.arange(NY, dtype=jnp.int32)) % NY
    query_tiles = src * NKT + kt
    key_tiles = y * NKT + jnp.arange(NKT, dtype=jnp.int32)
    hit_query = tile_pairs[None, :, 0] == query_tiles[:, None]
    hit_key = tile_pairs[None, :, 1] == key_tiles[:, None]
    live = jnp.any(hit_query[:, None, :] & hit_key[None, :, :], axis=2)
    head = tile_count // 8
    live = live & ((query_tiles < head)[:, None] | (key_tiles >= head)[None, :])
    live = live.astype(jnp.int32)
    busy = jnp.max(live, axis=1)
    meta = jnp.concatenate(
        [
            live,
            jnp.concatenate([y[None] * NKT, busy, jnp.zeros((NKT - 1 - NY,), jnp.int32)])[None],
            jnp.concatenate([query_tiles, jnp.zeros((NKT - NY,), jnp.int32)])[None],
            jnp.zeros((2, NKT), jnp.int32),
        ],
        axis=0,
    )

    hidden_swap = lax.ppermute(hidden, "kt", Z_SWAP)
    latent_part = jnp.dot(hidden, adapter_down, preferred_element_type=f32)

    dkv, dq0, dq1, dq2, dq3 = attend(meta, [blocks[s] for s in range(NY)], kv)

    dq_parts = []
    for (s, perm), part in zip(reversed(shifts), (dq3, dq2, dq1)):
        dq_parts.append(lax.ppermute(part, "qt", [(b, a) for a, b in perm]))
    query_grad = dq0
    for part in dq_parts:
        query_grad = query_grad + part.astype(f32)
    query_grad = query_grad.astype(bf16)

    dkv = lax.all_to_all(dkv, "kt", 0, 0, axis_index_groups=X_GROUPS, tiled=True)
    dkv = jnp.sum(dkv.astype(f32), axis=0)
    dkv_low = dkv.astype(bf16)
    dkv_swap = lax.ppermute(dkv_low, "kt", Z_SWAP)
    dkv_full = (dkv_low.astype(f32) + dkv_swap.astype(f32)).astype(bf16)

    back_part = jnp.concatenate(
        [
            jnp.einsum("ztc,rc->ztr", dkv_low[:, i], adapter_up[i], preferred_element_type=f32)
            for i in range(2)
        ],
        axis=2,
    )
    halves = jnp.concatenate([back_part, latent_part[None]], axis=0).reshape(NZ + 1, NCORE, TILE // NCORE, 2 * R)
    mine = lax.dynamic_index_in_dim(halves, core, 1, keepdims=False)
    other = lax.dynamic_index_in_dim(halves, 1 - core, 1, keepdims=False)
    got = lax.ppermute(other.astype(bf16), "hd", CORE_SWAP)
    half = (mine.astype(bf16).astype(f32) + got.astype(f32)).astype(bf16)
    ring = lax.all_to_all(
        jnp.broadcast_to(half[None], (NZ * NZLO,) + half.shape), ("kt", "hd"), 0, 0, axis_index_groups=Z_GROUPS, tiled=True
    ).astype(f32)
    back_half = jnp.sum(ring[:, :NZ], axis=0)
    latent_half = jnp.sum(ring[:, NZ].reshape(NZ, NZLO, TILE // NCORE, 2 * R), axis=1)
    both = jnp.stack([back_half, latent_half]).astype(bf16)
    both_other = lax.ppermute(both, "hd", CORE_SWAP)
    low_half = jnp.where(core == 0, both, both_other)
    high_half = jnp.where(core == 0, both_other, both)
    both = jnp.concatenate([low_half, high_half], axis=2).reshape(2, NZ * TILE, 2 * R)
    back_low, latent_low = both[0], both[1]

    hidden_both = jnp.concatenate(
        [jnp.where(z_hi == 0, hidden, hidden_swap), jnp.where(z_hi == 0, hidden_swap, hidden)], axis=0
    )
    down_piece = jnp.einsum("td,tr->dr", hidden_both, back_low, preferred_element_type=f32)
    up_pieces = [
        jnp.einsum(
            "tr,tc->rc",
            latent_low[:, i * R : (i + 1) * R],
            dkv_full[:, i].reshape(NZ * TILE, HD),
            preferred_element_type=f32,
        )
        for i in range(2)
    ]
    pieces = jnp.concatenate([down_piece] + up_pieces, axis=0).astype(bf16)
    count = NX * NY
    pieces = pieces.reshape(count, pieces.shape[0] // count, HD)
    pieces = lax.all_to_all(pieces, ("qt", "kt"), 0, 0, axis_index_groups=XY_GROUPS, tiled=True)
    total = (jnp.sum(pieces.astype(f32), axis=0) * SCALE).astype(bf16)
    total = lax.all_to_all(
        jnp.broadcast_to(total[None], (count,) + total.shape), ("qt", "kt"), 0, 0, axis_index_groups=XY_GROUPS, tiled=True
    )
    total = total.astype(f32).reshape(-1, HD)
    rows_down = hidden.shape[1]
    return (query_grad, total[:rows_down], total[rows_down:].reshape(2, R, HD))


def solution(mesh):
    return jax.shard_map(
        body,
        mesh=mesh,
        in_specs=(
            P(("qt", "kt"), "hd"),
            P(("qt", "kt"), "hd"),
            P(("qt", "kt"), "hd"),
            P(("qt", "kt"), "hd"),
            P("hd", ("qt", "kt")),
            P("hd", ("qt", "kt")),
            P(("qt", "kt")),
            P(),
            P(("qt", "kt"), "hd"),
            P("hd", None),
            P(None, None, "hd"),
        ),
        out_specs=(P(("qt", "kt"), "hd"), P("hd", None), P(None, None, "hd")),
        check_vma=False,
    )
```

```python
import functools
import math

import jax
import jax.numpy as jnp
from jax import lax
from jax.experimental import pallas as pl
from jax.experimental.pallas import tpu as pltpu
from jax.sharding import PartitionSpec as P


HD = 128
R = 64
TILE = 128
HEADS = 8
NY = 4
NX = 4
NZ = 2
NKT = NX * NZ
NZLO = 4
NCORE = 2
LOG2E = math.log2(math.e)
INV_ROOT = 1.0 / math.sqrt(HD)
SCALE = 0.25
ROWS = 2 * TILE + 16

f32 = jnp.float32
bf16 = jnp.bfloat16


def pack_kernel(q, o, log, delta, first, k, v, packed, kvs):
    packed[0:TILE, :] = q[...]
    packed[TILE : 2 * TILE, :] = o[...]

    def flat(x):
        return jnp.concatenate([x[h : h + 1, :] for h in range(HEADS)], axis=1)

    def split3(x):
        hi = x.astype(bf16).astype(f32)
        mid = (x - hi).astype(bf16).astype(f32)
        return [hi, mid, x - hi - mid]

    first_row = first[...].astype(f32)
    first_hi = first_row.astype(bf16).astype(f32)
    rows = split3(flat(log[...] * LOG2E)) + split3(flat(delta[...]))
    rows.append(jnp.concatenate([first_hi, first_row - first_hi, jnp.zeros((1, (HEADS - 2) * TILE), f32)], axis=1))
    rows.append(jnp.zeros((16 - len(rows), HEADS * TILE), f32))
    packed[2 * TILE : ROWS, :] = jnp.concatenate(rows, axis=0).astype(bf16)
    for t in range(NKT):
        kvs[t, 0:TILE, :] = k[...]
        kvs[t, TILE : 2 * TILE, :] = v[...]


def pack(q, o, log, delta, first, k, v):
    vm = pl.BlockSpec(memory_space=pltpu.VMEM)
    return pl.pallas_call(
        pack_kernel,
        in_specs=[vm] * 7,
        out_specs=[vm] * 2,
        out_shape=[pltpu.VMEM((ROWS, HEADS * HD), bf16), pltpu.VMEM((NKT, 2 * TILE, HD), bf16)],
        compiler_params=pltpu.CompilerParams(vmem_limit_bytes=16 << 20),
        name="pack",
    )(q, o, log, delta, first, k, v)


def attend_kernel(last, meta, pa, pb, kv, *refs):
    if last:
        acc_in, dkv, dqa, dqb, found, kt_sc, dq_sc, acc = refs
    else:
        acc, dqa, dqb, found, kt_sc, dq_sc = refs
    contract_last = (((1,), (1,)), ((), ()))
    if last:
        acc[...] = acc_in[...]
    else:
        acc[...] = jnp.zeros_like(acc)
    row = lax.broadcasted_iota(jnp.int32, (TILE, TILE), 0)
    col = lax.broadcasted_iota(jnp.int32, (TILE, TILE), 1)

    @pl.when(meta[2, 1] + meta[2, 2] > 0)
    def _():
        for t in range(NKT):
            kt_sc[t] = kv[t, 0:TILE, :].T

    for s, (p, dq) in enumerate(((pa, dqa), (pb, dqb))):

        @pl.when(meta[2, 1 + s] == 0)
        def _():
            dq[...] = jnp.zeros_like(dq)

        @pl.when(meta[2, 1 + s] > 0)
        def _():
            dq_sc[...] = jnp.zeros_like(dq_sc)
            rows = p[2 * TILE : ROWS, :].astype(f32)
            logs = rows[0:1] + rows[1:2] + rows[2:3]
            deltas = rows[3:4] + rows[4:5] + rows[5:6]
            first = (rows[6:7, 0:TILE] + rows[6:7, TILE : 2 * TILE]).astype(jnp.int32)
            query_pos = meta[2, 3 + s] * TILE + col

            def find(t, n):
                @pl.when(meta[s, t] > 0)
                def _():
                    found[n] = t

                return n + meta[s, t]

            count = lax.fori_loop(0, NKT, find, 0)
            found[count] = found[count - 1]

            queries = jnp.concatenate([p[0:TILE, h * HD : (h + 1) * HD] for h in range(HEADS)], axis=0)
            grads = jnp.concatenate([p[TILE : 2 * TILE, h * HD : (h + 1) * HD] for h in range(HEADS)], axis=0)

            def one_pair(i, carry):
                t0 = found[2 * i]
                t1 = found[2 * i + 1]
                key = jnp.concatenate([kv[t0, 0:TILE, :], kv[t1, 0:TILE, :]], axis=0)
                val = jnp.concatenate([kv[t0, TILE : 2 * TILE, :], kv[t1, TILE : 2 * TILE, :]], axis=0)
                trans = jnp.concatenate([kt_sc[t0], kt_sc[t1]], axis=1)
                tile1 = jnp.where(2 * i + 1 < count, meta[3, t1], NY * NKT)
                key_pos = jnp.concatenate([meta[3, t0] * TILE + row, tile1 * TILE + row], axis=0)
                allowed = (key_pos <= jnp.concatenate([query_pos] * 2, axis=0)) & (key_pos >= first)
                allowed = jnp.concatenate([allowed] * HEADS, axis=1)
                scores = lax.dot_general(key, queries, contract_last, preferred_element_type=f32)
                dprobs = lax.dot_general(val, grads, contract_last, preferred_element_type=f32)
                probs = jnp.where(allowed, jnp.exp2(scores * (INV_ROOT * LOG2E) - logs), 0.0)
                dscores = (probs * (dprobs - deltas)).astype(bf16)
                dval = jnp.dot(probs.astype(bf16), grads, preferred_element_type=f32)
                dkey = jnp.dot(dscores, queries, preferred_element_type=f32)
                for half, t in enumerate((t0, t1)):
                    rows_of = slice(half * TILE, (half + 1) * TILE)
                    acc[t, 1] += dval[rows_of]
                    acc[t, 0] += dkey[rows_of]
                dq_sc[...] += jnp.dot(trans, dscores, preferred_element_type=f32)
                return carry

            lax.fori_loop(0, (count + 1) // 2, one_pair, 0)
            for h in range(HEADS):
                cols = slice(h * HD, (h + 1) * HD)
                dq[:, cols] = (dq_sc[:, cols].T * INV_ROOT).astype(dq.dtype)

    if last:
        for t in range(NKT):
            dkv[t, 0] = (acc[t, 0] * INV_ROOT).astype(bf16)
            dkv[t, 1] = acc[t, 1].astype(bf16)


def attend(meta, pa, pb, kv, acc=None):
    last = acc is not None
    vm = pl.BlockSpec(memory_space=pltpu.VMEM)
    width = HEADS * HD
    acc_shape = (NKT, 2, TILE, HD)
    first_out = pltpu.VMEM((NKT, 2, TILE, HD), bf16) if last else pltpu.VMEM(acc_shape, f32)
    out_shape = [first_out, pltpu.VMEM((TILE, width), bf16 if last else f32), pltpu.VMEM((TILE, width), bf16)]
    scratch = [pltpu.SMEM((NKT + 1,), jnp.int32), pltpu.VMEM((NKT, HD, TILE), bf16), pltpu.VMEM((HD, HEADS * TILE), f32)]
    if last:
        scratch.append(pltpu.VMEM(acc_shape, f32))
    args = [pltpu.with_memory_space_constraint(x, pltpu.VMEM) for x in [pa, pb, kv] + ([acc] if last else [])]
    return pl.pallas_call(
        functools.partial(attend_kernel, last),
        in_specs=[pl.BlockSpec(memory_space=pltpu.SMEM)] + [vm] * len(args),
        out_specs=[vm] * 3,
        out_shape=out_shape,
        scratch_shapes=scratch,
        cost_estimate=pl.CostEstimate(flops=16 * 5 * 2 * HEADS * TILE**3, transcendentals=16 * HEADS * TILE**2, bytes_accessed=4 << 20),
        compiler_params=pltpu.CompilerParams(vmem_limit_bytes=28 << 20),
        name="attend_last" if last else "attend_first",
    )(meta, *args)


def groups(size, key):
    found = {}
    for i in range(size):
        found.setdefault(key(i), []).append(i)
    return list(found.values())


XY_GROUPS = groups(NY * NKT, lambda i: (i % NKT) // NX)
ZLO_GROUPS = groups(NZLO * NCORE, lambda i: i % NCORE)
Z_SWAP = [(i, i ^ NX) for i in range(NKT)]
CORE_SWAP = [(i, i ^ 1) for i in range(NZLO * NCORE)]


def whole(
    query_proj,
    key_proj,
    value_proj,
    out_grad,
    log_norm,
    row_delta,
    first_key,
    tile_pairs,
    hidden,
    adapter_down,
    adapter_up,
):
    y = lax.axis_index("qt")
    kt = lax.axis_index("kt")
    core = lax.axis_index("hd") % NCORE

    packed, kvs = pack(query_proj, out_grad, log_norm, row_delta, first_key.reshape(1, TILE), key_proj, value_proj)
    perms = {s: [(i, (i + s) % NY) for i in range(NY - s, NY)] for s in range(1, NY)}
    blocks = {0: packed}
    for s in (3, 2, 1):
        blocks[s] = lax.ppermute(packed, "qt", perms[s])
    kv = lax.all_to_all(kvs, "kt", 0, 0, tiled=True)

    def core_halves(x):
        x = x.reshape(x.shape[:-2] + (NCORE, TILE // NCORE, x.shape[-1]))
        pick = functools.partial(lax.dynamic_index_in_dim, x, axis=x.ndim - 3, keepdims=False)
        return pick(core), pick(1 - core)

    def core_join(mine, other):
        low = jnp.where(core == 0, mine, other)
        high = jnp.where(core == 0, other, mine)
        return jnp.concatenate([low, high], axis=-2)

    latent_part = jnp.dot(hidden, adapter_down, preferred_element_type=f32)

    tile_count = NY * NKT
    order = jnp.array([0, 3, 2, 1], jnp.int32)
    query_tiles = ((y - order) % NY) * NKT + kt
    key_tiles = y * NKT + jnp.arange(NKT, dtype=jnp.int32)
    hit_query = tile_pairs[None, :, 0] == query_tiles[:, None]
    hit_key = tile_pairs[None, :, 1] == key_tiles[:, None]
    live = jnp.any(hit_query[:, None, :] & hit_key[None, :, :], axis=2)
    head = tile_count // 8
    live = live & ((query_tiles < head)[:, None] | (key_tiles >= head)[None, :])
    live = live.astype(jnp.int32)
    busy = jnp.max(live, axis=1)
    base = (y * NKT)[None]
    pad = jnp.zeros((NKT - 5,), jnp.int32)
    metas = [
        jnp.concatenate([live[i : i + 2], jnp.concatenate([base, busy[i : i + 2], query_tiles[i : i + 2], pad])[None], key_tiles[None]], axis=0)
        for i in (0, 2)
    ]

    acc, dq0, dq3 = attend(metas[0], blocks[0], blocks[3], kv)
    dkv, dq2, dq1 = attend(metas[1], blocks[2], blocks[1], kv, acc)

    query_grad = dq0
    for s, part in ((3, dq3), (2, dq2), (1, dq1)):
        part = lax.ppermute(part, "qt", [(b, a) for a, b in perms[s]])
        query_grad = query_grad + part.astype(f32)
    query_grad = query_grad.astype(bf16)

    dkv = lax.all_to_all(dkv, "kt", 0, 0, tiled=True)
    dkv = jnp.sum(dkv.astype(f32), axis=0).astype(bf16)

    back_part = jnp.concatenate(
        [jnp.einsum("tc,rc->tr", dkv[i], adapter_up[i], preferred_element_type=f32) for i in range(2)], axis=1
    )
    mine, other = core_halves(jnp.stack([back_part, latent_part]))
    got = lax.ppermute(other.astype(bf16), "hd", CORE_SWAP)
    half = (mine + got.astype(f32)).astype(bf16)
    halves = jnp.broadcast_to(half[None], (NZLO,) + half.shape)
    ring = lax.all_to_all(halves, "hd", 0, 0, axis_index_groups=ZLO_GROUPS, tiled=True)
    half = jnp.sum(ring.astype(f32), axis=0).astype(bf16)
    both = core_join(half, lax.ppermute(half, "hd", CORE_SWAP))
    back_low, latent_low = both[0], both[1]

    down_piece = jnp.einsum("td,tr->dr", hidden, back_low, preferred_element_type=f32).astype(bf16)
    up_pieces = [
        jnp.einsum("tr,tc->rc", latent_low[:, i * R : (i + 1) * R], dkv[i], preferred_element_type=f32).astype(bf16)
        for i in range(2)
    ]
    up_piece = jnp.concatenate(up_pieces, axis=0)
    count = NX * NY
    pieces = jnp.concatenate([down_piece.reshape(count, -1, HD), up_piece.reshape(count, -1, HD)], axis=1)
    pieces = lax.all_to_all(pieces, ("qt", "kt"), 0, 0, axis_index_groups=XY_GROUPS, tiled=True)
    part = jnp.sum(pieces.astype(f32), axis=0).astype(bf16)
    part_other = lax.ppermute(part, "kt", Z_SWAP)
    total = ((part.astype(f32) + part_other.astype(f32)) * SCALE).astype(bf16)
    totals = jnp.broadcast_to(total[None], (count,) + total.shape)
    total = lax.all_to_all(totals, ("qt", "kt"), 0, 0, axis_index_groups=XY_GROUPS, tiled=True)
    rows_down = hidden.shape[1] // count
    down_factor = total[:, :rows_down].astype(f32).reshape(-1, HD)
    up_factor = total[:, rows_down:].astype(f32).reshape(2, R, HD)
    return (query_grad, down_factor, up_factor)


def solution(mesh):
    return jax.shard_map(
        whole,
        mesh=mesh,
        in_specs=(
            P(("qt", "kt"), "hd"),
            P(("qt", "kt"), "hd"),
            P(("qt", "kt"), "hd"),
            P(("qt", "kt"), "hd"),
            P("hd", ("qt", "kt")),
            P("hd", ("qt", "kt")),
            P(("qt", "kt")),
            P(),
            P(("qt", "kt"), "hd"),
            P("hd", None),
            P(None, None, "hd"),
        ),
        out_specs=(P(("qt", "kt"), "hd"), P("hd", None), P(None, None, "hd")),
        check_vma=False,
    )
```
